32 devices in a mesh: grid: 4 (over z), orb: 4 (over y, core), pts: 2 (over x).
Axes of the slice: x: 2, y: 2, z: 4, core: 2. Of those that a mesh axis runs over, the one named last changes fastest.
Arguments:
- orbitals: bfloat16 [1024, 2048], P('grid', 'orb'), may hold values from -6 to 6
- points: int32 [8192], replicated, may hold values from 0 to 1023
- fitting: bfloat16 [1024, 8192], P('grid', ('orb', 'pts')), may hold values from -0.0625 to 0.0625
- screened: bfloat16 [8192, 8192], P(('orb', 'pts'), 'grid'), may hold values from -0.0014648438 to 0.0014648438
Outputs:
- exchange_orbitals: float32 [2048, 1024], P(('orb', 'pts'), 'grid')
- exchange_matrix: float32 [2048, 2048], P(('orb', 'pts'), 'grid')
The draws below stay inside these ranges and needn't reach their ends.
Inputs may be any that keep to these rules, and one draw needn't show every extreme that they name: Grid rows of the window; two points may name the same row.
All inputs are finite; a program needn't handle non-finite values.
Results may differ from the reference program's by a relative error of at most 0.005.
Values may be sent and summed in bfloat16 or wider, within the bound.
A program may use at most 128 MiB of HBM per device.

```python
import math
import jax
import jax.numpy as jnp

NO = 2048
NP = 8192
NR = 1024


def place_ends(values, rng, low, largest):
    longest = values.shape.index(max(values.shape))
    spots = []
    for shift in (0, 1):
        where = [jax.random.randint(jax.random.fold_in(rng, axis), (), 0, length) for axis, length in enumerate(values.shape)]
        where[longest] = (where[longest] + shift) % values.shape[longest]
        spots.append(tuple(where))
    return values.at[spots[0]].set(low).at[spots[1]].set(largest)


def levels(rng, shape, split, low, high):
    def one(axis_at, blocks):
        heights = jax.random.uniform(jax.random.fold_in(jax.random.fold_in(rng, 6), axis_at), (blocks,), jnp.float32, low / len(split), high / len(split))
        return jnp.repeat(jnp.exp(heights), shape[axis_at] // blocks).reshape((-1,) + (1,) * (len(shape) - axis_at - 1))

    factor_of = one(*split[0])
    for cut in split[1:]:
        factor_of = factor_of * one(*cut)
    return factor_of


def scatter_about(rng, shape, scale, limit, cuts=(), held_as=jnp.bfloat16):
    array = jax.random.normal(rng, shape, jnp.float32) * scale
    if len(cuts) > 0:
        array = levels(rng, shape, cuts, -0.22, 0.18) * array
    return jnp.clip(array, min=-limit, max=limit).astype(held_as)


def setup_inputs(seed: int = 0) -> dict:
    streams_of = jax.random.split(jax.random.key(seed), 5)
    orbitals = scatter_about(streams_of[0], (NR, NO), 1.0, 6.0, ((0, 4), (1, 4)))
    points = place_ends(jax.random.randint(streams_of[1], (NP,), 0, NR), jax.random.fold_in(streams_of[1], 1), 0, NR - 1).astype(jnp.int32)
    fitting = scatter_about(streams_of[2], (NR, NP), NP ** -0.5, 0.0625, ((0, 4), (1, 8)))
    screened = scatter_about(streams_of[3], (NP, NP), (NP * NO) ** -0.5, 0.0014648438, ((0, 8), (1, 4)))
    return dict(orbitals=orbitals, points=points, fitting=fitting, screened=screened)


def reference(orbitals, points, fitting, screened):
    picked = jnp.take(orbitals, points.astype(jnp.int32), axis=0)
    density = jnp.dot(picked, picked.T, preferred_element_type=jnp.float32)
    masked = (density * screened.astype(jnp.float32)).astype(jnp.bfloat16)
    applied = jnp.dot(masked, picked, preferred_element_type=jnp.float32).astype(jnp.bfloat16)
    exchange = -jnp.dot(applied.T, fitting.T, preferred_element_type=jnp.float32)
    rounded = exchange.astype(jnp.bfloat16)
    summed = jnp.dot(rounded, orbitals, preferred_element_type=jnp.float32)
    matrix = summed / math.sqrt(NR)
    return (exchange, matrix)
```

```python
import math

import jax
import jax.numpy as jnp
from jax import lax
from jax.experimental import pallas as pl
from jax.experimental.pallas import tpu as pltpu
from jax.sharding import PartitionSpec as P

F32, BF16 = jnp.float32, jnp.bfloat16


def dot(a, b, ca, cb):
    return lax.dot_general(a, b, (((ca,), (cb,)), ((), ())), preferred_element_type=F32)


def middle(orb_ref, prow_ref, pcol_ref, fit_ref, scr_ref, v_ref, gram, rows, total):
    nrows = orb_ref.shape[0]
    npoint, ncol = scr_ref.shape
    tile = min(512, ncol)
    gtile = min(512, nrows)

    @pl.loop(0, nrows // gtile)
    def _(k):
        at = pl.ds(pl.multiple_of(k * gtile, gtile), gtile)
        gram[:, at] = dot(orb_ref[...], orb_ref[at, :], 1, 1).astype(BF16)

    hot = (lax.broadcasted_iota(jnp.int32, (npoint, nrows), 1) == prow_ref[...]).astype(F32)
    hot = hot.astype(BF16)

    @pl.loop(0, nrows // gtile)
    def _(k):
        at = pl.ds(pl.multiple_of(k * gtile, gtile), gtile)
        rows[:, at] = dot(hot, gram[:, at], 1, 0).astype(BF16)

    total[...] = jnp.zeros_like(total)

    @pl.loop(0, ncol // tile)
    def _(k):
        at = pl.ds(pl.multiple_of(k * tile, tile), tile)
        names = pcol_ref[:, at]
        pick = (lax.broadcasted_iota(jnp.int32, (nrows, tile), 0) == names).astype(F32).astype(BF16)
        density = dot(rows[...], pick, 1, 0)
        masked = (density * scr_ref[:, at].astype(F32)).astype(BF16)
        total[...] += dot(masked, pick, 1, 1)

    rows[...] = total[...].astype(BF16)

    @pl.loop(0, nrows // gtile)
    def _(k):
        at = pl.ds(pl.multiple_of(k * gtile, gtile), gtile)
        v_ref[:, at] = dot(fit_ref[...], rows[:, at], 1, 0)


def per_device(orbitals, points, fitting, screened):
    grid_index = lax.axis_index("grid")
    orb_index = lax.axis_index("orb")
    pts_index = lax.axis_index("pts")
    n_grid = lax.axis_size("grid")
    n_orb = lax.axis_size("orb")
    n_pts = lax.axis_size("pts")
    nrows = orbitals.shape[0] * n_grid
    width = orbitals.shape[1] * n_orb
    npoint, ncol = screened.shape
    block = orb_index * n_pts + pts_index
    full = lax.all_gather(
        lax.all_gather(orbitals, "orb", axis=1, tiled=True), "grid", axis=0, tiled=True
    )
    fit = lax.all_gather(fitting, "grid", axis=0, tiled=True)
    prow = lax.dynamic_slice_in_dim(points, block * npoint, npoint).reshape(npoint, 1)
    pcol = lax.dynamic_slice_in_dim(points, grid_index * ncol, ncol).reshape(1, ncol)
    v = pl.pallas_call(
        middle,
        out_shape=jax.ShapeDtypeStruct((nrows, nrows), F32),
        in_specs=[pl.BlockSpec(memory_space=pltpu.VMEM)] * 5,
        out_specs=pl.BlockSpec(memory_space=pltpu.VMEM),
        scratch_shapes=[
            pltpu.VMEM((nrows, nrows), BF16),
            pltpu.VMEM((npoint, nrows), BF16),
            pltpu.VMEM((npoint, nrows), F32),
        ],
        compiler_params=pltpu.CompilerParams(vmem_limit_bytes=60 * 2**20),
    )(full, prow, pcol, fit, screened)
    v = lax.psum_scatter(v, ("orb", "pts"), scatter_dimension=1, tiled=True)
    v = lax.psum_scatter(v, "grid", scatter_dimension=0, tiled=True).astype(BF16)
    v = lax.all_gather(v, ("orb", "pts"), axis=1, tiled=True)
    own = width // (n_orb * n_pts)
    mine = lax.dynamic_slice_in_dim(full, block * own, own, 1)
    terms = -dot(mine, v, 0, 1)
    rounded = lax.all_gather(terms.astype(BF16), "grid", axis=1, tiled=True)
    out_width = width // n_grid
    side = lax.dynamic_slice_in_dim(full, grid_index * out_width, out_width, 1)
    exchange_matrix = dot(rounded, side, 1, 0) / math.sqrt(nrows)
    return (terms, exchange_matrix)


def solution(mesh):
    in_specs = (P("grid", "orb"), P(), P("grid", ("orb", "pts")), P(("orb", "pts"), "grid"))
    out_specs = (P(("orb", "pts"), "grid"), P(("orb", "pts"), "grid"))
    return jax.shard_map(
        per_device, mesh=mesh, in_specs=in_specs, out_specs=out_specs, check_vma=False
    )
```

```python
import functools
import math

import jax
import jax.numpy as jnp
from jax import lax
from jax.experimental import pallas as pl
from jax.experimental.pallas import tpu as pltpu
from jax.sharding import PartitionSpec as P

F32, BF16 = jnp.float32, jnp.bfloat16
MESH = pl.DeviceIdType.MESH


def dot(a, b, ca, cb):
    return lax.dot_general(a, b, (((ca,), (cb,)), ((), ())), preferred_element_type=F32)


def span(start, size):
    return pl.ds(pl.multiple_of(start, size), size)


class Place:
    def __init__(self, sizes):
        self.nz, self.no, self.nx = sizes
        self.z = lax.axis_index("grid")
        self.o = lax.axis_index("orb")
        self.x = lax.axis_index("pts")
        self.core = lax.rem(self.o, 2)
        self.mate = self.o + 1 - 2 * self.core
        self.chips = (self.no // 2) * self.nx
        self.chip = (self.o // 2) * self.nx + self.x

    def other(self, j):
        c = lax.rem(self.chip + j, self.chips)
        return c, (c // self.nx) * 2 + self.core, lax.rem(c, self.nx)

    def at_mate(self):
        return {"orb": self.mate}


class Copies:
    def __init__(self):
        self.started = []

    def start(self, src, dst, send, recv, to, when=None):
        copy = pltpu.make_async_remote_copy(
            src_ref=src, dst_ref=dst, send_sem=send, recv_sem=recv, device_id=to, device_id_type=MESH
        )
        if when is None:
            copy.start()
        else:
            pl.when(when)(copy.start)
        self.started.append((copy, when))

    def finish(self):
        for copy, when in self.started:
            if when is None:
                copy.wait_send()
            else:
                pl.when(when)(copy.wait_send)


def arrived(dst, send, recv, to, when=None):
    copy = pltpu.make_async_remote_copy(
        src_ref=dst, dst_ref=dst, send_sem=send, recv_sem=recv, device_id=to, device_id_type=MESH
    )
    if when is None:
        copy.wait_recv()
    else:
        pl.when(when)(copy.wait_recv)


def first(sizes, orb_ref, prow_ref, pcol_ref, fit_ref, scr_ref, v_ref, mine_ref, side_ref,
          full, fit, gram, low, rows, rows_low, total, local_sem,
          o_recv, f_recv, right_sem, left_sem, plane_sem, mate_sem, f_right, f_left):
    me = Place(sizes)
    nz, chips, z = me.nz, me.chips, me.z
    deep, wide = orb_ref.shape
    half = deep // me.nx
    fdeep = fit_ref.shape[0]

    barrier = pltpu.get_barrier_semaphore()

    def greet(to):
        pl.semaphore_signal(barrier, inc=1, device_id=to, device_id_type=MESH)

    has_right, has_left = z < nz - 1, z > 0
    pl.when(has_right)(lambda: greet({"grid": z + 1}))
    pl.when(has_left)(lambda: greet({"grid": z - 1}))
    greet(me.at_mate())
    for j in range(1, chips):
        _, o, x = me.other(j)
        greet({"orb": o, "pts": x})
    pl.semaphore_wait(barrier, chips + has_right.astype(jnp.int32) + has_left.astype(jnp.int32))

    copies = Copies()

    def spot(zz, o, x):
        return full.at[span(zz * deep + x * half, half), span(o * wide, wide)]

    own_half = orb_ref.at[span(me.x * half, half), :]
    own_local = pltpu.make_async_copy(own_half, spot(z, me.o, me.x), local_sem.at[0])
    own_local.start()
    fit_local = pltpu.make_async_copy(fit_ref, fit.at[span(z * fdeep, fdeep), :], local_sem.at[1])
    fit_local.start()

    def plane(zz, src, s, when):
        for j in range(1, chips):
            _, o, x = me.other(j)
            copies.start(src, spot(zz, me.o, me.x), plane_sem.at[s, j], o_recv.at[zz, me.o, me.x],
                         {"orb": o, "pts": x}, when)

    def wait_piece(zz, o, x, when=None):
        arrived(spot(zz, o, x), local_sem.at[2], o_recv.at[zz, o, x], me.at_mate(), when)

    sides = []
    here = spot(z, me.o, me.x)
    copies.start(own_half, here, right_sem.at[0], o_recv.at[z, me.o, me.x], {"grid": z + 1}, has_right)
    copies.start(own_half, here, left_sem.at[0], o_recv.at[z, me.o, me.x], {"grid": z - 1}, has_left)
    plane(z, own_half, 0, None)
    for s in range(1, nz):
        lo, hi = jnp.maximum(z - s, 0), jnp.minimum(z + s, nz - 1)
        in_lo, in_hi = z - s >= 0, z + s < nz
        for zz, here_too, sem, to, onward in (
            (lo, in_lo, right_sem, z + 1, has_right), (hi, in_hi, left_sem, z - 1, has_left)
        ):
            wait_piece(zz, me.o, me.x, here_too)
            src = spot(zz, me.o, me.x)
            copies.start(src, src, sem.at[s], o_recv.at[zz, me.o, me.x], {"grid": to},
                         here_too & onward)
        plane(lo, spot(lo, me.o, me.x), 2 * s - 1, in_lo)
        plane(hi, spot(hi, me.o, me.x), 2 * s, in_hi)

    fit_here = fit.at[span(z * fdeep, fdeep), :]
    copies.start(fit_ref, fit_here, f_right.at[0], f_recv.at[z], {"grid": z + 1}, has_right)
    copies.start(fit_ref, fit_here, f_left.at[0], f_recv.at[z], {"grid": z - 1}, has_left)

    def pass_fit(s):
        for zz, here_too, sem, to, onward in (
            (jnp.maximum(z - s, 0), z - s >= 0, f_right, z + 1, has_right),
            (jnp.minimum(z + s, nz - 1), z + s < nz, f_left, z - 1, has_left),
        ):
            src = fit.at[span(zz * fdeep, fdeep), :]
            arrived(src, local_sem.at[2], f_recv.at[zz], me.at_mate(), here_too)
            copies.start(src, src, sem.at[s], f_recv.at[zz], {"grid": to}, here_too & onward)

    own_local.wait()
    for d in range(nz):
        zz = lax.rem(z + d, nz)
        for j in range(chips):
            _, o, x = me.other(j)
            if j > 0:
                wait_piece(zz, o, x)
            src = spot(zz, o, x)
            copies.start(src, src, mate_sem.at[d, j], o_recv.at[zz, o, x], me.at_mate())
    for d in range(nz):
        zz = lax.rem(z + d, nz)
        for j in range(chips):
            _, o, x = me.other(j)
            wait_piece(zz, o + 1 - 2 * me.core, x)

    if nz > 1:
        pass_fit(1)

    nrows = full.shape[0]
    npoint, ncol = scr_ref.shape
    tile = min(512, ncol)
    gtile = min(512, nrows)

    @pl.loop(0, nrows // gtile)
    def _(k):
        at = span(k * gtile, gtile)
        value = dot(full[...], full[at, :], 1, 1)
        rounded = value.astype(BF16)
        gram[:, at] = rounded
        low[:, at] = (value - rounded.astype(F32)).astype(BF16)

    hot = (lax.broadcasted_iota(jnp.int32, (npoint, nrows), 1) == prow_ref[...]).astype(F32)
    hot = hot.astype(BF16)

    @pl.loop(0, nrows // gtile)
    def _(k):
        at = span(k * gtile, gtile)
        rows[:, at] = dot(hot, gram[:, at], 1, 0).astype(BF16)
        rows_low[:, at] = dot(hot, low[:, at], 1, 0).astype(BF16)

    for s in range(2, nz):
        pass_fit(s)

    total[...] = jnp.zeros_like(total)

    @pl.loop(0, ncol // tile)
    def _(k):
        at = span(k * tile, tile)
        names = pcol_ref[:, at]
        pick = (lax.broadcasted_iota(jnp.int32, (nrows, tile), 0) == names).astype(F32).astype(BF16)
        density = dot(rows[...], pick, 1, 0) + dot(rows_low[...], pick, 1, 0)
        masked = (density * scr_ref[:, at].astype(F32)).astype(BF16)
        total[...] += dot(masked, pick, 1, 1)

    rows[...] = total[...].astype(BF16)
    own = mine_ref.shape[1]
    number = me.o * me.nx + me.x
    if own >= 128:
        mine_ref[...] = full[:, span(number * own, own)]
    else:
        parts = 128 // own
        block = full[:, span((number // parts) * 128, 128)]
        for k in range(parts):

            @pl.when(lax.rem(number, parts) == k)
            def _(k=k):
                mine_ref[...] = block[:, k * own : (k + 1) * own]

    own = side_ref.shape[1]
    side_ref[...] = full[:, span(z * own, own)]
    fit_local.wait()

    @pl.loop(0, nrows // gtile)
    def _(k):
        at = span(k * gtile, gtile)
        v_ref[:, at] = dot(fit[...], rows[:, at], 1, 0)

    copies.finish()


def second(sizes, v_ref, mine_ref, side_ref, terms_ref, matrix_ref,
           core_in, send, kept, plane_in, z_send, z_in, whole, rounded, dummy,
           core_s, core_r, plane_s, plane_r, z_s, z_r, w_s, w_r, m_s, e_s, e_r):
    me = Place(sizes)
    nz, chips, z = me.nz, me.chips, me.z
    nrows = v_ref.shape[0]
    deep = nrows // nz
    sub = deep // chips
    wide = nrows // 2

    barrier = pltpu.get_barrier_semaphore()

    def greet(to):
        pl.semaphore_signal(barrier, inc=1, device_id=to, device_id_type=MESH)

    greet(me.at_mate())
    for j in range(1, chips):
        _, o, x = me.other(j)
        greet({"orb": o, "pts": x})
    for d in range(1, nz):
        greet({"grid": lax.rem(z + d, nz)})
    pl.semaphore_wait(barrier, chips + nz - 1)

    copies = Copies()

    def got(dst, recv):
        arrived(dst, dummy.at[0], recv, me.at_mate())

    mine_cols, mate_cols = span(me.core * wide, wide), span((1 - me.core) * wide, wide)
    order = [(d, lax.rem(z + d, nz)) for d in range(1, nz + 1)]
    for d, zz in order:
        at = span(zz * deep, deep)
        copies.start(v_ref.at[at, mate_cols], core_in.at[at, :], core_s.at[d - 1], core_r.at[d - 1],
                     me.at_mate())
    for d, zz in order:
        at = span(zz * deep, deep)
        got(core_in.at[at, :], core_r.at[d - 1])
        for j in range(chips):
            c, o, x = me.other(j)
            part = span(zz * deep + c * sub, sub)
            value = v_ref[part, mine_cols] + core_in[part, :]
            if j == 0:
                kept[d - 1] = value
            else:
                send[d - 1, j - 1] = value.astype(BF16)
                copies.start(send.at[d - 1, j - 1], plane_in.at[d - 1, j - 1],
                             plane_s.at[d - 1, j - 1], plane_r.at[d - 1, j - 1], {"orb": o, "pts": x})
    for d, zz in order:
        value = kept[d - 1]
        for j in range(1, chips):
            got(plane_in.at[d - 1, j - 1], plane_r.at[d - 1, j - 1])
            value = value + plane_in[d - 1, j - 1].astype(F32)
        if d < nz:
            z_send[d - 1] = value.astype(BF16)
            copies.start(z_send.at[d - 1], z_in.at[d - 1], z_s.at[d - 1], z_r.at[d - 1], {"grid": zz})
    for d in range(1, nz):
        got(z_in.at[d - 1], z_r.at[d - 1])
        value = value + z_in[d - 1].astype(F32)

    def piece(c, core):
        return whole.at[span(c * sub, sub), span(core * wide, wide)]

    whole[span(me.chip * sub, sub), mine_cols] = value.astype(BF16)
    own_piece = piece(me.chip, me.core)
    for j in range(1, chips):
        _, o, x = me.other(j)
        copies.start(own_piece, own_piece, w_s.at[j - 1], w_r.at[me.chip, me.core], {"orb": o, "pts": x})
    for j in range(chips):
        c, _, _ = me.other(j)
        src = piece(c, me.core)
        if j > 0:
            got(src, w_r.at[c, me.core])
        copies.start(src, src, m_s.at[j], w_r.at[c, me.core], me.at_mate())
    for j in range(chips):
        c, _, _ = me.other(j)
        got(piece(c, 1 - me.core), w_r.at[c, 1 - me.core])

    exchange = -dot(mine_ref[...], whole[...], 0, 1)
    terms_ref[...] = exchange
    rounded[z] = exchange.astype(BF16)
    for d in range(1, nz):
        copies.start(rounded.at[z], rounded.at[z], e_s.at[d - 1], e_r.at[z],
                     {"grid": lax.rem(z + d, nz)})
    total = dot(rounded[z], side_ref[span(z * deep, deep), :], 1, 0)
    for d in range(1, nz):
        zz = lax.rem(z + d, nz)
        got(rounded.at[zz], e_r.at[zz])
        total = total + dot(rounded[zz], side_ref[span(zz * deep, deep), :], 1, 0)
    matrix_ref[...] = total / math.sqrt(nrows)
    copies.finish()


def per_device(orbitals, points, fitting, screened):
    grid_index = lax.axis_index("grid")
    block = lax.axis_index("orb") * lax.axis_size("pts") + lax.axis_index("pts")
    sizes = nz, no, nx = lax.axis_size("grid"), lax.axis_size("orb"), lax.axis_size("pts")
    nrows = orbitals.shape[0] * nz
    width = orbitals.shape[1] * no
    npoint, ncol = screened.shape
    chips = (no // 2) * nx
    prow = lax.dynamic_slice_in_dim(points, block * npoint, npoint).reshape(npoint, 1)
    pcol = lax.dynamic_slice_in_dim(points, grid_index * ncol, ncol).reshape(1, ncol)
    vmem = pl.BlockSpec(memory_space=pltpu.VMEM)
    dma = pltpu.SemaphoreType.DMA
    own, out_width = width // (no * nx), width // nz
    v, mine, side = pl.pallas_call(
        functools.partial(first, sizes),
        out_shape=(
            jax.ShapeDtypeStruct((nrows, nrows), F32),
            jax.ShapeDtypeStruct((nrows, own), BF16),
            jax.ShapeDtypeStruct((nrows, out_width), BF16),
        ),
        in_specs=[vmem] * 5,
        out_specs=(vmem,) * 3,
        scratch_shapes=[
            pltpu.VMEM((nrows, width), BF16),
            pltpu.VMEM((nrows, npoint), BF16),
            pltpu.VMEM((nrows, nrows), BF16),
            pltpu.VMEM((nrows, nrows), BF16),
            pltpu.VMEM((npoint, nrows), BF16),
            pltpu.VMEM((npoint, nrows), BF16),
            pltpu.VMEM((npoint, nrows), F32),
            dma((3,)),
            dma((nz, no, nx)),
            dma((nz,)),
            dma((nz,)),
            dma((nz,)),
            dma((2 * nz, chips)),
            dma((nz, chips)),
            dma((nz,)),
            dma((nz,)),
        ],
        compiler_params=pltpu.CompilerParams(
            collective_id=0, has_side_effects=True, vmem_limit_bytes=60 * 2**20
        ),
    )(orbitals, prow, pcol, fitting, screened)
    deep = nrows // nz
    sub, wide = deep // chips, nrows // 2
    others = max(chips - 1, 1)
    return pl.pallas_call(
        functools.partial(second, sizes),
        out_shape=(
            jax.ShapeDtypeStruct((own, deep), F32),
            jax.ShapeDtypeStruct((own, out_width), F32),
        ),
        in_specs=[vmem] * 3,
        out_specs=(vmem,) * 2,
        scratch_shapes=[
            pltpu.VMEM((nrows, wide), F32),
            pltpu.VMEM((nz, others, sub, wide), BF16),
            pltpu.VMEM((nz, sub, wide), F32),
            pltpu.VMEM((nz, others, sub, wide), BF16),
            pltpu.VMEM((nz, sub, wide), BF16),
            pltpu.VMEM((nz, sub, wide), BF16),
            pltpu.VMEM((deep, nrows), BF16),
            pltpu.VMEM((nz, own, deep), BF16),
            dma((1,)),
            dma((nz,)),
            dma((nz,)),
            dma((nz, others)),
            dma((nz, others)),
            dma((nz,)),
            dma((nz,)),
            dma((others,)),
            dma((chips, 2)),
            dma((chips,)),
            dma((nz,)),
            dma((nz,)),
        ],
        compiler_params=pltpu.CompilerParams(
            collective_id=1, has_side_effects=True, vmem_limit_bytes=60 * 2**20
        ),
    )(v, mine, side)


def solution(mesh):
    in_specs = (P("grid", "orb"), P(), P("grid", ("orb", "pts")), P(("orb", "pts"), "grid"))
    out_specs = (P(("orb", "pts"), "grid"), P(("orb", "pts"), "grid"))
    return jax.shard_map(
        per_device, mesh=mesh, in_specs=in_specs, out_specs=out_specs, check_vma=False
    )
```

```python
import functools
import math

import jax
import jax.numpy as jnp
from jax import lax
from jax.experimental import pallas as pl
from jax.experimental.pallas import tpu as pltpu
from jax.sharding import PartitionSpec as P

F32, BF16 = jnp.float32, jnp.bfloat16
MESH = pl.DeviceIdType.MESH


def dot(a, b, ca, cb):
    return lax.dot_general(a, b, (((ca,), (cb,)), ((), ())), preferred_element_type=F32)


def span(start, size):
    return pl.ds(pl.multiple_of(start, size), size)


class Place:
    def __init__(self, sizes):
        self.nz, self.no, self.nx = sizes
        self.z = lax.axis_index("grid")
        self.o = lax.axis_index("orb")
        self.x = lax.axis_index("pts")
        self.core = lax.rem(self.o, 2)
        self.mate = self.o + 1 - 2 * self.core
        self.chips = (self.no // 2) * self.nx
        self.chip = (self.o // 2) * self.nx + self.x

    def other(self, j):
        c = lax.rem(self.chip + j, self.chips)
        return c, (c // self.nx) * 2 + self.core, lax.rem(c, self.nx)

    def at_mate(self):
        return {"orb": self.mate}


class Copies:
    def __init__(self):
        self.started = []

    def start(self, src, dst, send, recv, to, when=None):
        copy = pltpu.make_async_remote_copy(
            src_ref=src, dst_ref=dst, send_sem=send, recv_sem=recv, device_id=to, device_id_type=MESH
        )
        if when is None:
            copy.start()
        else:
            pl.when(when)(copy.start)
        self.started.append((copy, when))

    def finish(self):
        for copy, when in self.started:
            if when is None:
                copy.wait_send()
            else:
                pl.when(when)(copy.wait_send)


def arrived(dst, send, recv, to, when=None):
    copy = pltpu.make_async_remote_copy(
        src_ref=dst, dst_ref=dst, send_sem=send, recv_sem=recv, device_id=to, device_id_type=MESH
    )
    if when is None:
        copy.wait_recv()
    else:
        pl.when(when)(copy.wait_recv)


def fused(sizes, orb_ref, points_ref, fit_ref, scr_ref, terms_ref, matrix_ref,
          full, fit, gram, low, rows, rows_low, total, mine, v_mate, v_own, core_in, send, plane_in,
          z_send, z_in, exchange, local_sem,
          o_recv, f_recv, right_sem, left_sem, plane_sem, mate_sem, f_sem,
          core_s, core_r, plane_s, plane_r, z_s, z_r, w_z, w_p, w_m, w_r):
    me = Place(sizes)
    nz, chips, z = me.nz, me.chips, me.z
    deep, wide = orb_ref.shape
    half = deep // me.nx

    barrier = pltpu.get_barrier_semaphore()

    def greet(to):
        pl.semaphore_signal(barrier, inc=1, device_id=to, device_id_type=MESH)

    greet(me.at_mate())
    for j in range(1, chips):
        _, o, x = me.other(j)
        greet({"orb": o, "pts": x})
    for d in range(1, nz):
        greet({"grid": lax.rem(z + d, nz)})
    pl.semaphore_wait(barrier, chips + nz - 1)

    has_right, has_left = z < nz - 1, z > 0
    copies = Copies()

    def got(dst, recv, when=None):
        arrived(dst, local_sem.at[2], recv, me.at_mate(), when)

    def spot(zz, o, x):
        return full.at[span(zz * deep + x * half, half), span(o * wide, wide)]

    own_half = orb_ref.at[span(me.x * half, half), :]
    own_local = pltpu.make_async_copy(own_half, spot(z, me.o, me.x), local_sem.at[0])
    own_local.start()
    fit_local = pltpu.make_async_copy(fit_ref, fit.at[span(z * deep, deep), :], local_sem.at[1])
    fit_local.start()

    def plane(zz, src, s, when):
        for j in range(1, chips):
            _, o, x = me.other(j)
            copies.start(src, spot(zz, me.o, me.x), plane_sem.at[s, j], o_recv.at[zz, me.o, me.x],
                         {"orb": o, "pts": x}, when)

    def wait_piece(zz, o, x, when=None):
        got(spot(zz, o, x), o_recv.at[zz, o, x], when)

    here = spot(z, me.o, me.x)
    copies.start(own_half, here, right_sem.at[0], o_recv.at[z, me.o, me.x], {"grid": z + 1}, has_right)
    copies.start(own_half, here, left_sem.at[0], o_recv.at[z, me.o, me.x], {"grid": z - 1}, has_left)
    plane(z, own_half, 0, None)
    for s in range(1, nz):
        lo, hi = jnp.maximum(z - s, 0), jnp.minimum(z + s, nz - 1)
        in_lo, in_hi = z - s >= 0, z + s < nz
        for zz, here_too, sem, to, onward in (
            (lo, in_lo, right_sem, z + 1, has_right), (hi, in_hi, left_sem, z - 1, has_left)
        ):
            wait_piece(zz, me.o, me.x, here_too)
            src = spot(zz, me.o, me.x)
            copies.start(src, src, sem.at[s], o_recv.at[zz, me.o, me.x], {"grid": to},
                         here_too & onward)
        plane(lo, spot(lo, me.o, me.x), 2 * s - 1, in_lo)
        plane(hi, spot(hi, me.o, me.x), 2 * s, in_hi)

    for d in range(1, nz):
        copies.start(fit_ref, fit.at[span(z * deep, deep), :], f_sem.at[d], f_recv.at[z],
                     {"grid": lax.rem(z + d, nz)})

    own_local.wait()
    for d in range(nz):
        zz = lax.rem(z + d, nz)
        for j in range(chips):
            _, o, x = me.other(j)
            if j > 0:
                wait_piece(zz, o, x)
            src = spot(zz, o, x)
            copies.start(src, src, mate_sem.at[d, j], o_recv.at[zz, o, x], me.at_mate())
    for d in range(nz):
        zz = lax.rem(z + d, nz)
        for j in range(chips):
            _, o, x = me.other(j)
            wait_piece(zz, o + 1 - 2 * me.core, x)

    nrows = full.shape[0]
    npoint, ncol = scr_ref.shape
    tile = min(512, ncol)
    gtile = min(512, nrows)
    number = me.o * me.nx + me.x

    @pl.loop(0, nrows // gtile)
    def _(k):
        at = span(k * gtile, gtile)
        value = dot(full[...], full[at, :], 1, 1)
        rounded = value.astype(BF16)
        gram[:, at] = rounded
        low[:, at] = (value - rounded.astype(F32)).astype(BF16)

    names = points_ref[:, span(number * npoint, npoint)].astype(F32)
    names = jnp.transpose(jnp.broadcast_to(names, (128, npoint)))[:, :1]
    hot = (lax.broadcasted_iota(jnp.int32, (npoint, nrows), 1) == names.astype(jnp.int32))
    hot = hot.astype(F32).astype(BF16)

    @pl.loop(0, nrows // gtile)
    def _(k):
        at = span(k * gtile, gtile)
        rows[:, at] = dot(hot, gram[:, at], 1, 0).astype(BF16)
        rows_low[:, at] = dot(hot, low[:, at], 1, 0).astype(BF16)

    total[...] = jnp.zeros_like(total)

    @pl.loop(0, ncol // tile)
    def _(k):
        at = span(k * tile, tile)
        names = points_ref[:, span(z * ncol + k * tile, tile)]
        pick = (lax.broadcasted_iota(jnp.int32, (nrows, tile), 0) == names).astype(F32).astype(BF16)
        density = dot(rows[...], pick, 1, 0) + dot(rows_low[...], pick, 1, 0)
        masked = (density * scr_ref[:, at].astype(F32)).astype(BF16)
        total[...] += dot(masked, pick, 1, 1)

    rows[...] = total[...].astype(BF16)
    own = mine.shape[1]
    if own >= 128:
        mine[...] = full[:, span(number * own, own)]
    else:
        parts = 128 // own
        block = full[:, span((number // parts) * 128, 128)]
        for k in range(parts):

            @pl.when(lax.rem(number, parts) == k)
            def _(k=k):
                mine[...] = block[:, k * own : (k + 1) * own]

    sub, wide = deep // chips, nrows // 2
    mine_cols, mate_cols = span(me.core * wide, wide), span((1 - me.core) * wide, wide)
    order = [(d, lax.rem(z + d, nz)) for d in range(1, nz + 1)]
    for d, zz in order:
        at = span(zz * deep, deep)
        if d < nz:
            got(fit.at[at, :], f_recv.at[zz])
        else:
            fit_local.wait()
        v_mate[d - 1] = dot(fit[at, :], rows[:, mate_cols], 1, 0).astype(BF16)
        copies.start(v_mate.at[d - 1], core_in.at[d - 1], core_s.at[d - 1], core_r.at[d - 1], me.at_mate())
        v_own[d - 1] = dot(fit[at, :], rows[:, mine_cols], 1, 0)
    for d, zz in order:
        got(core_in.at[d - 1], core_r.at[d - 1])
        for j in list(range(1, chips)) + [0]:
            c, o, x = me.other(j)
            part = span(c * sub, sub)
            value = v_own[d - 1, part, :] + core_in[d - 1, part, :].astype(F32)
            if j == 0:
                v_own[d - 1, part, :] = value
            else:
                send[d - 1, j - 1] = value.astype(BF16)
                copies.start(send.at[d - 1, j - 1], plane_in.at[d - 1, j - 1],
                             plane_s.at[d - 1, j - 1], plane_r.at[d - 1, j - 1], {"orb": o, "pts": x})
    for d, zz in order:
        value = v_own[d - 1, span(me.chip * sub, sub), :]
        for j in range(1, chips):
            got(plane_in.at[d - 1, j - 1], plane_r.at[d - 1, j - 1])
            value = value + plane_in[d - 1, j - 1].astype(F32)
        if d < nz:
            z_send[d - 1] = value.astype(BF16)
            copies.start(z_send.at[d - 1], z_in.at[d - 1], z_s.at[d - 1], z_r.at[d - 1], {"grid": zz})
    for d in range(1, nz):
        got(z_in.at[d - 1], z_r.at[d - 1])
        value = value + z_in[d - 1].astype(F32)

    def piece(zz, c, core):
        return gram.at[span(zz * deep + c * sub, sub), span(core * wide, wide)]

    def pass_on(zz, d, j):
        c, _, _ = me.other(j)
        src = piece(zz, c, me.core)
        copies.start(src, src, w_m.at[d, j], w_r.at[zz, c, me.core], me.at_mate())

    gram[span(z * deep + me.chip * sub, sub), mine_cols] = value.astype(BF16)
    own_piece = piece(z, me.chip, me.core)
    for d in range(1, nz):
        copies.start(own_piece, own_piece, w_z.at[d], w_r.at[z, me.chip, me.core],
                     {"grid": lax.rem(z + d, nz)})
    for d in range(nz):
        zz = lax.rem(z + d, nz)
        src = piece(zz, me.chip, me.core)
        if d > 0:
            got(src, w_r.at[zz, me.chip, me.core])
        for j in range(1, chips):
            _, o, x = me.other(j)
            copies.start(src, src, w_p.at[d, j], w_r.at[zz, me.chip, me.core], {"orb": o, "pts": x})
        pass_on(zz, d, 0)
    for d in range(nz):
        zz = lax.rem(z + d, nz)
        for j in range(1, chips):
            c, _, _ = me.other(j)
            got(piece(zz, c, me.core), w_r.at[zz, c, me.core])
            pass_on(zz, d, j)
    for d in range(nz):
        zz = lax.rem(z + d, nz)
        for j in range(chips):
            c, _, _ = me.other(j)
            got(piece(zz, c, 1 - me.core), w_r.at[zz, c, 1 - me.core])

    exchange[...] = -dot(mine[...], gram[...], 0, 1)
    terms_ref[...] = exchange[:, span(z * deep, deep)]
    out = matrix_ref.shape[1]
    matrix_ref[...] = dot(exchange[...].astype(BF16), full[:, span(z * out, out)], 1, 0)
    copies.finish()


def finish(nrows, terms_ref, matrix_ref, terms_out, matrix_out):
    terms_out[...] = terms_ref[...]
    matrix_out[...] = matrix_ref[...] / math.sqrt(nrows)


def per_device(orbitals, points, fitting, screened):
    sizes = nz, no, nx = lax.axis_size("grid"), lax.axis_size("orb"), lax.axis_size("pts")
    deep, columns = orbitals.shape
    nrows, width = deep * nz, columns * no
    npoint, ncol = screened.shape
    chips = (no // 2) * nx
    vmem = pl.BlockSpec(memory_space=pltpu.VMEM)
    dma = pltpu.SemaphoreType.DMA
    own, out_width = width // (no * nx), width // nz
    sub, wide = deep // chips, nrows // 2
    others = max(chips - 1, 1)
    outs = (
        jax.ShapeDtypeStruct((own, deep), F32),
        jax.ShapeDtypeStruct((own, out_width), F32),
    )
    results = pl.pallas_call(
        functools.partial(fused, sizes),
        out_shape=outs,
        in_specs=[vmem] * 4,
        out_specs=(vmem,) * 2,
        scratch_shapes=[
            pltpu.VMEM((nrows, width), BF16),
            pltpu.VMEM((nrows, npoint), BF16),
            pltpu.VMEM((nrows, nrows), BF16),
            pltpu.VMEM((nrows, nrows), BF16),
            pltpu.VMEM((npoint, nrows), BF16),
            pltpu.VMEM((npoint, nrows), BF16),
            pltpu.VMEM((npoint, nrows), F32),
            pltpu.VMEM((nrows, own), BF16),
            pltpu.VMEM((nz, deep, wide), BF16),
            pltpu.VMEM((nz, deep, wide), F32),
            pltpu.VMEM((nz, deep, wide), BF16),
            pltpu.VMEM((nz, others, sub, wide), BF16),
            pltpu.VMEM((nz, others, sub, wide), BF16),
            pltpu.VMEM((nz, sub, wide), BF16),
            pltpu.VMEM((nz, sub, wide), BF16),
            pltpu.VMEM((own, nrows), F32),
            dma((3,)),
            dma((nz, no, nx)),
            dma((nz,)),
            dma((nz,)),
            dma((nz,)),
            dma((2 * nz, chips)),
            dma((nz, chips)),
            dma((nz,)),
            dma((nz,)),
            dma((nz,)),
            dma((nz, others)),
            dma((nz, others)),
            dma((nz,)),
            dma((nz,)),
            dma((nz,)),
            dma((nz, chips)),
            dma((nz, chips)),
            dma((nz, chips, 2)),
        ],
        compiler_params=pltpu.CompilerParams(
            collective_id=0, has_side_effects=True, vmem_limit_bytes=63 * 2**20
        ),
    )(orbitals, points.reshape(1, -1), fitting, screened)
    return pl.pallas_call(
        functools.partial(finish, nrows),
        out_shape=outs,
        in_specs=[vmem] * 2,
        out_specs=(vmem,) * 2,
    )(*results)


def solution(mesh):
    in_specs = (P("grid", "orb"), P(), P("grid", ("orb", "pts")), P(("orb", "pts"), "grid"))
    out_specs = (P(("orb", "pts"), "grid"), P(("orb", "pts"), "grid"))
    return jax.shard_map(
        per_device, mesh=mesh, in_specs=in_specs, out_specs=out_specs, check_vma=False
    )
```

```python
import functools
import math

import jax
import jax.numpy as jnp
from jax import lax
from jax.experimental import pallas as pl
from jax.experimental.pallas import tpu as pltpu
from jax.sharding import PartitionSpec as P

F32, BF16 = jnp.float32, jnp.bfloat16
MESH = pl.DeviceIdType.MESH


def dot(a, b, ca, cb):
    return lax.dot_general(a, b, (((ca,), (cb,)), ((), ())), preferred_element_type=F32)


def span(start, size):
    return pl.ds(pl.multiple_of(start, size), size)


class Place:
    def __init__(self, sizes):
        self.nz, self.no, self.nx = sizes
        self.z = lax.axis_index("grid")
        self.o = lax.axis_index("orb")
        self.x = lax.axis_index("pts")
        self.core = lax.rem(self.o, 2)
        self.mate = self.o + 1 - 2 * self.core
        self.chips = (self.no // 2) * self.nx
        self.chip = (self.o // 2) * self.nx + self.x

    def other(self, j):
        c = lax.rem(self.chip + j, self.chips)
        return c, (c // self.nx) * 2 + self.core, lax.rem(c, self.nx)

    def peer(self, ja, jx):
        a = lax.rem(self.o // 2 + ja, self.no // 2)
        x = lax.rem(self.x + jx, self.nx)
        return a * self.nx + x, a * 2 + self.core, x

    def peers(self):
        near = [(0, jx) for jx in range(1, self.nx)] + [(ja, 0) for ja in range(1, self.no // 2)]
        far = [(ja, jx) for ja in range(1, self.no // 2) for jx in range(1, self.nx)]
        return near + far, []

    def onward(self, d, ja, jx):
        if False:
            return [(k, jx, k, 0) for k in range(1, self.no // 2)]
        if False:
            return [(ja, k, 0, k) for k in range(1, self.nx)]
        return []

    def at_mate(self):
        return {"orb": self.mate}


class Copies:
    def __init__(self):
        self.started = []

    def start(self, src, dst, send, recv, to, when=None):
        copy = pltpu.make_async_remote_copy(
            src_ref=src, dst_ref=dst, send_sem=send, recv_sem=recv, device_id=to, device_id_type=MESH
        )
        if when is None:
            copy.start()
        else:
            pl.when(when)(copy.start)
        self.started.append((copy, when))

    def finish(self):
        for copy, when in self.started:
            if when is None:
                copy.wait_send()
            else:
                pl.when(when)(copy.wait_send)


def arrived(dst, send, recv, to, when=None):
    copy = pltpu.make_async_remote_copy(
        src_ref=dst, dst_ref=dst, send_sem=send, recv_sem=recv, device_id=to, device_id_type=MESH
    )
    if when is None:
        copy.wait_recv()
    else:
        pl.when(when)(copy.wait_recv)


def fused(sizes, orb_ref, points_ref, fit_ref, scr_any, terms_ref, matrix_ref,
          scr_ref, full, fit, gram, low, rows, rows_low, total, mine, v_mate, v_own, core_in, send, plane_in,
          z_send, z_in, exchange, local_sem,
          o_recv, f_recv, right_sem, left_sem, plane_sem, mate_sem, f_sem, onward_sem, relay_sem,
          core_s, core_r, plane_s, plane_r, z_s, z_r, w_z, w_p, w_m, w_r):
    me = Place(sizes)
    nz, chips, z = me.nz, me.chips, me.z
    deep, wide = orb_ref.shape
    half = deep // me.nx

    barrier = pltpu.get_barrier_semaphore()

    def greet(to):
        pl.semaphore_signal(barrier, inc=1, device_id=to, device_id_type=MESH)

    greet(me.at_mate())
    for j in range(1, chips):
        _, o, x = me.other(j)
        greet({"orb": o, "pts": x})
    for d in range(1, nz):
        greet({"grid": lax.rem(z + d, nz)})
    pl.semaphore_wait(barrier, chips + nz - 1)

    has_right, has_left = z < nz - 1, z > 0
    copies = Copies()
    near, far = me.peers()

    def got(dst, recv, when=None):
        arrived(dst, local_sem.at[2], recv, me.at_mate(), when)

    def spot(zz, o, x):
        return full.at[span(zz * deep + x * half, half), span(o * wide, wide)]

    own_half = orb_ref.at[span(me.x * half, half), :]
    own_local = pltpu.make_async_copy(own_half, spot(z, me.o, me.x), local_sem.at[0])
    own_local.start()
    fit_local = pltpu.make_async_copy(fit_ref, fit.at[span(z * deep, deep), :], local_sem.at[1])
    fit_local.start()
    scr_local = pltpu.make_async_copy(scr_any, scr_ref, local_sem.at[3])
    scr_local.start()

    def plane(zz, src, s, when):
        for ja, jx in near:
            _, o, x = me.peer(ja, jx)
            copies.start(src, spot(zz, me.o, me.x), plane_sem.at[s, ja * me.nx + jx], o_recv.at[zz, me.o, me.x],
                         {"orb": o, "pts": x}, when)

    def wait_piece(zz, o, x, when=None):
        got(spot(zz, o, x), o_recv.at[zz, o, x], when)

    here = spot(z, me.o, me.x)
    copies.start(own_half, here, right_sem.at[0], o_recv.at[z, me.o, me.x], {"grid": z + 1}, has_right)
    copies.start(own_half, here, left_sem.at[0], o_recv.at[z, me.o, me.x], {"grid": z - 1}, has_left)
    plane(z, own_half, 0, None)
    for s in range(1, nz):
        lo, hi = jnp.maximum(z - s, 0), jnp.minimum(z + s, nz - 1)
        in_lo, in_hi = z - s >= 0, z + s < nz
        for zz, here_too, sem, to, onward in (
            (lo, in_lo, right_sem, z + 1, has_right), (hi, in_hi, left_sem, z - 1, has_left)
        ):
            wait_piece(zz, me.o, me.x, here_too)
            src = spot(zz, me.o, me.x)
            copies.start(src, src, sem.at[s], o_recv.at[zz, me.o, me.x], {"grid": to},
                         here_too & onward)
        plane(lo, spot(lo, me.o, me.x), 2 * s - 1, in_lo)
        plane(hi, spot(hi, me.o, me.x), 2 * s, in_hi)

    for d in range(1, nz):
        to = lax.rem(z + d, nz)
        relayed = ((to == nz - 1) & (z == nz - 3)) | ((to == 0) & (z == 2))
        copies.start(fit_ref, fit.at[span(z * deep, deep), :], f_sem.at[d], f_recv.at[z],
                     {"grid": to}, jnp.logical_not(relayed))
    has_relay_right, has_relay_left = (z == nz - 2) & (z >= 1), (z == 1) & (nz >= 3)

    def relay(origin, to, k, when):
        src = fit.at[span(origin * deep, deep), :]
        got(src, f_recv.at[origin], when)
        copies.start(src, src, relay_sem.at[k], f_recv.at[origin], {"grid": to}, when)

    own_local.wait()
    for d in range(nz):
        zz = lax.rem(z + d, nz)
        for ja, jx in [(0, 0)] + near:
            _, o, x = me.peer(ja, jx)
            if (ja, jx) != (0, 0):
                wait_piece(zz, o, x)
            src = spot(zz, o, x)
            for fa, fx, ka, kx in me.onward(d, ja, jx):
                _, oo, xx = me.peer(ka, kx)
                copies.start(src, src, onward_sem.at[d, fa * me.nx + fx], o_recv.at[zz, o, x],
                             {"orb": oo, "pts": xx})
            copies.start(src, src, mate_sem.at[d, ja * me.nx + jx], o_recv.at[zz, o, x], me.at_mate())
    for d in range(nz):
        zz = lax.rem(z + d, nz)
        for ja, jx in far:
            _, o, x = me.peer(ja, jx)
            wait_piece(zz, o, x)
            src = spot(zz, o, x)
            copies.start(src, src, mate_sem.at[d, ja * me.nx + jx], o_recv.at[zz, o, x], me.at_mate())
    for d in range(nz):
        zz = lax.rem(z + d, nz)
        for j in range(chips):
            _, o, x = me.other(j)
            wait_piece(zz, o + 1 - 2 * me.core, x)

    nrows = full.shape[0]
    npoint, ncol = scr_ref.shape
    tile = min(1024, ncol)
    gtile = min(512, nrows)
    number = me.o * me.nx + me.x

    @pl.loop(0, nrows // gtile)
    def _(k):
        at = span(k * gtile, gtile)
        value = dot(full[...], full[at, :], 1, 1)
        rounded = value.astype(BF16)
        gram[:, at] = rounded
        low[:, at] = (value - rounded.astype(F32)).astype(BF16)

    names = points_ref[:, span(number * npoint, npoint)].astype(F32)
    names = jnp.transpose(jnp.broadcast_to(names, (128, npoint)))[:, :1]
    hot = (lax.broadcasted_iota(jnp.int32, (npoint, nrows), 1) == names.astype(jnp.int32))
    hot = hot.astype(F32).astype(BF16)

    @pl.loop(0, nrows // gtile)
    def _(k):
        at = span(k * gtile, gtile)
        rows[:, at] = dot(hot, gram[:, at], 1, 0).astype(BF16)
        rows_low[:, at] = dot(hot, low[:, at], 1, 0).astype(BF16)

    if nz >= 3:
        relay(nz - 3, nz - 1, 0, has_relay_right)
        relay(2, 0, 1, has_relay_left)
    total[...] = jnp.zeros_like(total)
    scr_local.wait()

    @pl.loop(0, ncol // tile)
    def _(k):
        at = span(k * tile, tile)
        names = points_ref[:, span(z * ncol + k * tile, tile)]
        pick = (lax.broadcasted_iota(jnp.int32, (nrows, tile), 0) == names).astype(F32).astype(BF16)
        density = dot(rows[...], pick, 1, 0) + dot(rows_low[...], pick, 1, 0)
        masked = (density * scr_ref[:, at].astype(F32)).astype(BF16)
        total[...] += dot(masked, pick, 1, 1)

    rows[...] = total[...].astype(BF16)
    own = mine.shape[1]
    if own >= 128:
        mine[...] = full[:, span(number * own, own)]
    else:
        parts = 128 // own
        block = full[:, span((number // parts) * 128, 128)]
        for k in range(parts):

            @pl.when(lax.rem(number, parts) == k)
            def _(k=k):
                mine[...] = block[:, k * own : (k + 1) * own]

    sub, wide = deep // chips, nrows // 2
    mine_cols, mate_cols = span(me.core * wide, wide), span((1 - me.core) * wide, wide)
    order = [(d, lax.rem(z + d, nz)) for d in range(1, nz + 1)]
    for d, zz in order:
        at = span(zz * deep, deep)
        if d < nz:
            taken = ((zz == nz - 3) & has_relay_right) | ((zz == 2) & has_relay_left)
            got(fit.at[at, :], f_recv.at[zz], jnp.logical_not(taken))
        else:
            fit_local.wait()
        v_mate[d - 1] = dot(fit[at, :], rows[:, mate_cols], 1, 0).astype(BF16)
        copies.start(v_mate.at[d - 1], core_in.at[d - 1], core_s.at[d - 1], core_r.at[d - 1], me.at_mate())
        v_own[d - 1] = dot(fit[at, :], rows[:, mine_cols], 1, 0)
    for d, zz in order:
        got(core_in.at[d - 1], core_r.at[d - 1])
        for j in list(range(1, chips)) + [0]:
            c, o, x = me.other(j)
            part = span(c * sub, sub)
            value = v_own[d - 1, part, :] + core_in[d - 1, part, :].astype(F32)
            if j == 0:
                v_own[d - 1, part, :] = value
            else:
                send[d - 1, j - 1] = value.astype(BF16)
                copies.start(send.at[d - 1, j - 1], plane_in.at[d - 1, j - 1],
                             plane_s.at[d - 1, j - 1], plane_r.at[d - 1, j - 1], {"orb": o, "pts": x})
    for d, zz in order:
        value = v_own[d - 1, span(me.chip * sub, sub), :]
        for j in range(1, chips):
            got(plane_in.at[d - 1, j - 1], plane_r.at[d - 1, j - 1])
            value = value + plane_in[d - 1, j - 1].astype(F32)
        if d < nz:
            z_send[d - 1] = value.astype(BF16)
            copies.start(z_send.at[d - 1], z_in.at[d - 1], z_s.at[d - 1], z_r.at[d - 1], {"grid": zz})
    for d in range(1, nz):
        got(z_in.at[d - 1], z_r.at[d - 1])
        value = value + z_in[d - 1].astype(F32)

    def piece(zz, c, core):
        return gram.at[span(zz * deep + c * sub, sub), span(core * wide, wide)]

    def pass_on(zz, d, ja, jx):
        c, _, _ = me.peer(ja, jx)
        src = piece(zz, c, me.core)
        for fa, fx, ka, kx in me.onward(d, ja, jx):
            _, oo, xx = me.peer(ka, kx)
            copies.start(src, src, w_p.at[d, fa * me.nx + fx], w_r.at[zz, c, me.core],
                         {"orb": oo, "pts": xx})
        copies.start(src, src, w_m.at[d, ja * me.nx + jx], w_r.at[zz, c, me.core], me.at_mate())

    gram[span(z * deep + me.chip * sub, sub), mine_cols] = value.astype(BF16)
    own_piece = piece(z, me.chip, me.core)
    for d in range(1, nz):
        copies.start(own_piece, own_piece, w_z.at[d], w_r.at[z, me.chip, me.core],
                     {"grid": lax.rem(z + d, nz)})
    for d in range(nz):
        zz = lax.rem(z + d, nz)
        src = piece(zz, me.chip, me.core)
        if d > 0:
            got(src, w_r.at[zz, me.chip, me.core])
        for ja, jx in near:
            _, o, x = me.peer(ja, jx)
            copies.start(src, src, w_p.at[d, ja * me.nx + jx], w_r.at[zz, me.chip, me.core], {"orb": o, "pts": x})
        pass_on(zz, d, 0, 0)
    for group in (near, far):
        for d in range(nz):
            zz = lax.rem(z + d, nz)
            for ja, jx in group:
                c, _, _ = me.peer(ja, jx)
                got(piece(zz, c, me.core), w_r.at[zz, c, me.core])
                pass_on(zz, d, ja, jx)
    for d in range(nz):
        zz = lax.rem(z + d, nz)
        for j in range(chips):
            c, _, _ = me.other(j)
            got(piece(zz, c, 1 - me.core), w_r.at[zz, c, 1 - me.core])

    exchange[...] = -dot(mine[...], gram[...], 0, 1)
    terms_ref[...] = exchange[:, span(z * deep, deep)]
    out = matrix_ref.shape[1]
    matrix_ref[...] = dot(exchange[...].astype(BF16), full[:, span(z * out, out)], 1, 0)
    copies.finish()


def finish(nrows, terms_ref, matrix_ref, terms_out, matrix_out):
    terms_out[...] = terms_ref[...]
    matrix_out[...] = matrix_ref[...] / math.sqrt(nrows)


def per_device(orbitals, points, fitting, screened):
    sizes = nz, no, nx = lax.axis_size("grid"), lax.axis_size("orb"), lax.axis_size("pts")
    deep, columns = orbitals.shape
    nrows, width = deep * nz, columns * no
    npoint, ncol = screened.shape
    chips = (no // 2) * nx
    vmem = pl.BlockSpec(memory_space=pltpu.VMEM)
    dma = pltpu.SemaphoreType.DMA
    own, out_width = width // (no * nx), width // nz
    sub, wide = deep // chips, nrows // 2
    others = max(chips - 1, 1)
    outs = (
        jax.ShapeDtypeStruct((own, deep), F32),
        jax.ShapeDtypeStruct((own, out_width), F32),
    )
    results = pl.pallas_call(
        functools.partial(fused, sizes),
        out_shape=outs,
        in_specs=[vmem] * 3 + [pl.BlockSpec(memory_space=pl.ANY)],
        out_specs=(vmem,) * 2,
        scratch_shapes=[
            pltpu.VMEM((npoint, ncol), BF16),
            pltpu.VMEM((nrows, width), BF16),
            pltpu.VMEM((nrows, npoint), BF16),
            pltpu.VMEM((nrows, nrows), BF16),
            pltpu.VMEM((nrows, nrows), BF16),
            pltpu.VMEM((npoint, nrows), BF16),
            pltpu.VMEM((npoint, nrows), BF16),
            pltpu.VMEM((npoint, nrows), F32),
            pltpu.VMEM((nrows, own), BF16),
            pltpu.VMEM((nz, deep, wide), BF16),
            pltpu.VMEM((nz, deep, wide), F32),
            pltpu.VMEM((nz, deep, wide), BF16),
            pltpu.VMEM((nz, others, sub, wide), BF16),
            pltpu.VMEM((nz, others, sub, wide), BF16),
            pltpu.VMEM((nz, sub, wide), BF16),
            pltpu.VMEM((nz, sub, wide), BF16),
            pltpu.VMEM((own, nrows), F32),
            dma((4,)),
            dma((nz, no, nx)),
            dma((nz,)),
            dma((nz,)),
            dma((nz,)),
            dma((2 * nz, chips)),
            dma((nz, chips)),
            dma((nz,)),
            dma((nz, chips)),
            dma((2,)),
            dma((nz,)),
            dma((nz,)),
            dma((nz, others)),
            dma((nz, others)),
            dma((nz,)),
            dma((nz,)),
            dma((nz,)),
            dma((nz, chips)),
            dma((nz, chips)),
            dma((nz, chips, 2)),
        ],
        compiler_params=pltpu.CompilerParams(
            collective_id=0, has_side_effects=True, vmem_limit_bytes=63 * 2**20
        ),
    )(orbitals, points.reshape(1, -1), fitting, screened)
    return pl.pallas_call(
        functools.partial(finish, nrows),
        out_shape=outs,
        in_specs=[vmem] * 2,
        out_specs=(vmem,) * 2,
    )(*results)


def solution(mesh):
    in_specs = (P("grid", "orb"), P(), P("grid", ("orb", "pts")), P(("orb", "pts"), "grid"))
    out_specs = (P(("orb", "pts"), "grid"), P(("orb", "pts"), "grid"))
    return jax.shard_map(
        per_device, mesh=mesh, in_specs=in_specs, out_specs=out_specs, check_vma=False
    )
```
